32 devices in a mesh: section: 2 (over x), frame: 4 (over z), head: 4 (over y, core).
Axes of the slice: x: 2, y: 2, z: 4, core: 2. Of those that a mesh axis runs over, the one named last changes fastest.
Arguments:
- inputs: bfloat16 [2, 2, 16, 128, 3072], P('section', None, 'frame'), may hold values from -45 to 45
- upstream: bfloat16 [2, 16, 128, 3072], P(None, 'frame'), may hold values from -6 to 6
- norm_gain: float32 [2, 3072], P('section'), may hold values from 0.5 to 2
- head_gain: float32 [2, 2, 128], P('section'), may hold values from 0.5 to 2
- w_query: bfloat16 [2, 3072, 3072], P('section', 'frame', 'head'), may hold values from -0.109375 to 0.109375
- w_key: bfloat16 [2, 3072, 3072], P('section', 'frame', 'head'), may hold values from -0.109375 to 0.109375
- w_value: bfloat16 [2, 3072, 3072], P('section', 'frame', 'head'), may hold values from -0.109375 to 0.109375
- w_out: bfloat16 [2, 3072, 3072], P('section', 'head', 'frame'), may hold values from -0.109375 to 0.109375
Outputs:
- input_grads: bfloat16 [2, 2, 16, 128, 3072], P('section', None, 'frame', None, 'head')
The draws below stay inside these ranges and needn't reach their ends.
All inputs are finite; a program needn't handle non-finite values.
Results may differ from the reference program's by a relative error of at most 0.014.
Values may be sent and summed in bfloat16 or wider, within the bound.
No kernel may reach another device: no remote copies, remote signals or barrier semaphores. Data moves between devices by JAX's collectives and lax.ppermute only.
A program may use at most 192 MiB of HBM per device.

```python
import math
import jax
import jax.numpy as jnp
from jax import lax

D = 3072
HEAD_DIM = 128
FRAMES = 16
PATCHES = 128
MB = 2
HH = 3072
NFR = 16
VIDEOS = 1
N_HEAD = 4


def draw_inputs(key, part):
    shape_full = (2, MB, NFR, PATCHES, D)
    key_base, key_rows, key_cols = jax.random.split(key, 3)
    row_scale = jnp.exp(jax.random.uniform(key_rows, (2, MB, NFR, PATCHES, 1), minval=-1.15, maxval=1.15))
    col_scale = jnp.exp(jax.random.uniform(key_cols, (2, 1, 1, 1, D), minval=-1.15, maxval=1.15))
    base = jnp.clip(jax.random.normal(key_base, shape_full), -3.0, 3.0)
    return (base * row_scale * col_scale).astype(jnp.bfloat16)


def block_levels(rng, dims, cuts, smallest, largest):
    factor_of, own = 1.0, jax.random.fold_in(rng, 6)
    for position, blocks in cuts:
        steps = jnp.exp(jax.random.uniform(jax.random.fold_in(own, position), (blocks,), jnp.float32, smallest / len(cuts), largest / len(cuts)))
        factor_of = factor_of * jnp.repeat(steps, dims[position] // blocks).reshape([-1 if axis == position else 1 for axis in range(len(dims))])
    return factor_of


def scatter_about(key, extent, spread, limit, cuts=(), dtype=jnp.bfloat16):
    values = spread * jax.random.normal(key, extent, jnp.float32)
    if cuts:
        values = values * block_levels(key, extent, cuts, -0.22, 0.18)
    return jnp.clip(values, -limit, limit).astype(dtype)


def setup_inputs(seed: int = 0) -> dict:
    key_of = jax.random.split(jax.random.key(seed), 9)
    inputs = draw_inputs(jax.random.fold_in(key_of[8], 71), 0)
    upstream = scatter_about(key_of[1], (MB, NFR, PATCHES, D), 1.0, 6.0, ((1, 4),))
    norm_gain = jnp.clip(jnp.exp(math.log(2.0) - 1.3862944 * jax.random.uniform(key_of[2], (2, D), jnp.float32) ** block_levels(key_of[2], (2, D), ((0, 2),), -0.2, 0.2)), 0.5, 2.0)
    head_gain = jnp.clip(jnp.exp(math.log(2.0) - 1.3862944 * jax.random.uniform(key_of[3], (2, 2, HEAD_DIM), jnp.float32) ** block_levels(key_of[3], (2, 2, HEAD_DIM), ((0, 2),), -0.2, 0.2)), 0.5, 2.0)
    w_query = scatter_about(key_of[4], (2, D, HH), D ** -0.5, 0.109375, ((0, 2), (1, 4), (2, 4)))
    w_key = scatter_about(key_of[5], (2, D, HH), D ** -0.5, 0.109375, ((0, 2), (1, 4), (2, 4)))
    w_value = scatter_about(key_of[6], (2, D, HH), D ** -0.5, 0.109375, ((0, 2), (1, 4), (2, 4)))
    w_out = scatter_about(key_of[7], (2, HH, D), HH ** -0.5, 0.109375, ((0, 2), (1, 4), (2, 4)))
    return dict(inputs=inputs, upstream=upstream, norm_gain=norm_gain, head_gain=head_gain, w_query=w_query, w_key=w_key, w_value=w_value, w_out=w_out)


EPS = 1e-06

def attend_back(query_low, key_rows, value_low, grad_out):
    query_wide = query_low.astype(jnp.float32)
    key_wide = key_rows.astype(jnp.float32)
    value_wide = value_low.astype(jnp.float32)
    grad_wide = grad_out.astype(jnp.float32)
    scores = jnp.einsum('blhd,bmhd->bhlm', query_wide, key_wide)
    expo_scores = jnp.exp(scores)
    probs_full = expo_scores / lax.optimization_barrier(jnp.sum(expo_scores, axis=-1, keepdims=True))
    probs_low = probs_full.astype(jnp.bfloat16)
    grad_probs = jnp.einsum('blhd,bmhd->bhlm', grad_wide, value_wide)
    inner_sum = lax.optimization_barrier(jnp.sum(probs_full * grad_probs, axis=-1, keepdims=True))
    dscore = (probs_full * (grad_probs - inner_sum)).astype(jnp.bfloat16)
    dscore_wide = dscore.astype(jnp.float32)
    dquery = jnp.einsum('bhlm,bmhd->blhd', dscore_wide, key_wide)
    grad_key = jnp.einsum('bhlm,blhd->bmhd', dscore_wide, query_wide)
    dvalue = jnp.einsum('bhlm,blhd->bmhd', probs_low.astype(jnp.float32), grad_wide)
    return (dquery.astype(jnp.bfloat16), grad_key.astype(jnp.bfloat16), dvalue.astype(jnp.bfloat16))

def head_norm(raw_rows):
    scale_rows = lax.rsqrt(lax.optimization_barrier(jnp.mean(raw_rows * raw_rows, axis=-1, keepdims=True)) + EPS)
    return (raw_rows * scale_rows, scale_rows)

def norm_back(grad_low, normal_hat, scale_rows, gain_vec):
    grad_hat = grad_low.astype(jnp.float32) * gain_vec
    inner_mean = lax.optimization_barrier(jnp.mean(grad_hat * normal_hat, axis=-1, keepdims=True))
    return (scale_rows * (grad_hat - normal_hat * inner_mean)).astype(jnp.bfloat16)

def to_time(array_in, patch_count, heads_total):
    shaped = array_in.reshape(VIDEOS, FRAMES, patch_count, heads_total, HEAD_DIM)
    return shaped.transpose(0, 2, 1, 3, 4).reshape(VIDEOS * patch_count, FRAMES, heads_total, HEAD_DIM)

def from_time(array_in, patch_count, heads_total):
    shaped = array_in.reshape(VIDEOS, patch_count, FRAMES, heads_total, HEAD_DIM)
    return shaped.transpose(0, 2, 1, 3, 4).reshape(VIDEOS * FRAMES, patch_count, heads_total, HEAD_DIM)

def sublayer_back(saved_rows, grad_rows, gain_row, head_gains, query_weight, key_weight, value_weight, out_weight, temporal):
    frame_count, patch_count, feat_width = saved_rows.shape
    row_count = frame_count * patch_count
    heads_total = query_weight.shape[1] // HEAD_DIM
    flat_rows = saved_rows.reshape(row_count, feat_width).astype(jnp.float32)
    inv_rms = lax.rsqrt(lax.optimization_barrier(jnp.mean(flat_rows * flat_rows, axis=-1, keepdims=True)) + EPS)
    normed = flat_rows * inv_rms
    normed_low = (normed * gain_row).astype(jnp.bfloat16)

    def project(weight):
        return jnp.dot(normed_low, weight, preferred_element_type=jnp.float32).reshape(frame_count, patch_count, heads_total, HEAD_DIM)
    query_raw = project(query_weight)
    key_raw = project(key_weight)
    value_low = project(value_weight).astype(jnp.bfloat16)
    query_hat, query_scale = head_norm(query_raw)
    key_hat, key_scale = head_norm(key_raw)
    query_gain = head_gains[0] * HEAD_DIM ** (-0.5)
    query_low = (query_hat * query_gain).astype(jnp.bfloat16)
    key_low = (key_hat * head_gains[1]).astype(jnp.bfloat16)
    grad_flat = grad_rows.reshape(row_count, feat_width)
    grad_attn = jnp.dot(grad_flat, out_weight.T, preferred_element_type=jnp.float32)
    grad_attn = grad_attn.astype(jnp.bfloat16).reshape(frame_count, patch_count, heads_total, HEAD_DIM)
    if temporal:
        dquery, grad_key, dvalue = attend_back(to_time(query_low, patch_count, heads_total), to_time(key_low, patch_count, heads_total), to_time(value_low, patch_count, heads_total), to_time(grad_attn, patch_count, heads_total))
        dquery = from_time(dquery, patch_count, heads_total)
        grad_key = from_time(grad_key, patch_count, heads_total)
        dvalue = from_time(dvalue, patch_count, heads_total)
    else:
        dquery, grad_key, dvalue = attend_back(query_low, key_low, value_low, grad_attn)
    dquery_raw = norm_back(dquery, query_hat, query_scale, query_gain)
    dkey_raw = norm_back(grad_key, key_hat, key_scale, head_gains[1])
    per_group = heads_total // N_HEAD
    summed = jnp.zeros((row_count, feat_width), jnp.float32)
    for group_index in range(N_HEAD):
        first = group_index * per_group

        def group_part(grad_low, weight):
            cols = grad_low[:, :, first:first + per_group].reshape(row_count, per_group * HEAD_DIM)
            block = weight[:, first * HEAD_DIM:(first + per_group) * HEAD_DIM]
            return jnp.dot(cols, block.T, preferred_element_type=jnp.float32)
        dnorm = group_part(dquery_raw, query_weight) + group_part(dkey_raw, key_weight) + group_part(dvalue, value_weight)
        grad_hat = dnorm * gain_row
        term_rows = inv_rms * (grad_hat - normed * lax.optimization_barrier(jnp.mean(grad_hat * normed, axis=-1, keepdims=True)))
        term_low = lax.optimization_barrier(term_rows.astype(jnp.bfloat16))
        summed = summed + term_low.astype(jnp.float32)
    result = (grad_flat.astype(jnp.float32) + summed).astype(jnp.bfloat16)
    return result.reshape(frame_count, patch_count, feat_width)

def reference(inputs, upstream, norm_gain, head_gain, w_query, w_key, w_value, w_out):
    spatial_list = []
    temporal_list = []
    for batch_index in range(MB):
        spatial = sublayer_back(inputs[1, batch_index], upstream[batch_index], norm_gain[1], head_gain[1], w_query[1], w_key[1], w_value[1], w_out[1], False)
        temporal = sublayer_back(inputs[0, batch_index], spatial, norm_gain[0], head_gain[0], w_query[0], w_key[0], w_value[0], w_out[0], True)
        spatial_list.append(spatial)
        temporal_list.append(temporal)
    return jnp.stack([jnp.stack(temporal_list), jnp.stack(spatial_list)])
```

```python
import functools

import jax
import jax.numpy as jnp
from jax import lax
from jax.experimental import pallas as pl
from jax.experimental.pallas import tpu as pltpu
from jax.sharding import PartitionSpec as P

FRAMES = 16
EPS = 1e-06


def dot_nn(left, right):
    return lax.dot_general(left, right, (((1,), (0,)), ((), ())), preferred_element_type=jnp.float32)


def dot_nt(left, right):
    return lax.dot_general(left, right, (((1,), (1,)), ((), ())), preferred_element_type=jnp.float32)


def dot_tn(left, right):
    return lax.dot_general(left, right, (((0,), (0,)), ((), ())), preferred_element_type=jnp.float32)


def head_norm(raw_rows):
    scale_rows = lax.rsqrt(jnp.mean(raw_rows * raw_rows, axis=-1, keepdims=True) + EPS)
    return raw_rows * scale_rows, scale_rows


def norm_back(grad_low, normal_hat, scale_rows, gain_vec):
    grad_hat = grad_low.astype(jnp.float32) * gain_vec
    inner_mean = jnp.mean(grad_hat * normal_hat, axis=-1, keepdims=True)
    return (scale_rows * (grad_hat - normal_hat * inner_mean)).astype(jnp.bfloat16)


def attend_back(query_low, key_low, value_low, grad_attn, mask):
    expo = jnp.exp(dot_nt(query_low, key_low)) * mask
    probs = expo / jnp.sum(expo, axis=-1, keepdims=True)
    dprob = dot_nt(grad_attn, value_low)
    dscore = (probs * (dprob - jnp.sum(probs * dprob, axis=-1, keepdims=True))).astype(jnp.bfloat16)
    dquery = dot_nn(dscore, key_low).astype(jnp.bfloat16)
    dkey = dot_tn(dscore, query_low).astype(jnp.bfloat16)
    dvalue = dot_tn(probs.astype(jnp.bfloat16), grad_attn).astype(jnp.bfloat16)
    return dquery, dkey, dvalue


def chunk_kernel(first, last, width, head_dim, block, *refs):
    mask_ref, gains_ref, low_ref, grad_ref, weight_ref = refs[:5]
    refs = refs[5:]
    if not first:
        total_ref, refs = refs[0], refs[1:]
    if last:
        saved_ref, inv_ref, gain_ref = refs[:3]
        refs = refs[3:]
    out_ref, packed_ref = refs
    rows = low_ref.shape[0]
    query_gain, key_gain = gains_ref[0:1, :], gains_ref[1:2, :]
    mask = mask_ref[...]
    query_raw = dot_nn(low_ref[...], weight_ref[:, 0:width])
    key_raw = dot_nn(low_ref[...], weight_ref[:, width : 2 * width])
    value = dot_nn(low_ref[...], weight_ref[:, 2 * width : 3 * width]).astype(jnp.bfloat16)
    grad_attn = dot_nn(grad_ref[...], weight_ref[:, 3 * width : 4 * width]).astype(jnp.bfloat16)
    for head in range(width // head_dim):
        cols = slice(head * head_dim, (head + 1) * head_dim)
        query_hat, query_scale = head_norm(query_raw[:, cols])
        key_hat, key_scale = head_norm(key_raw[:, cols])
        query_low = (query_hat * query_gain).astype(jnp.bfloat16)
        key_low = (key_hat * key_gain).astype(jnp.bfloat16)
        for part in range(rows // block):
            own = slice(part * block, (part + 1) * block)
            dquery, dkey, dvalue = attend_back(
                query_low[own], key_low[own], value[own, cols], grad_attn[own, cols], mask
            )
            packed_ref[own, cols] = norm_back(dquery, query_hat[own], query_scale[own], query_gain)
            packed_ref[own, width + cols.start : width + cols.stop] = norm_back(
                dkey, key_hat[own], key_scale[own], key_gain
            )
            packed_ref[own, 2 * width + cols.start : 2 * width + cols.stop] = dvalue
    dnorm = dot_nt(packed_ref[...], weight_ref[:, 0 : 3 * width])
    if not first:
        dnorm = dnorm + total_ref[...]
    if not last:
        out_ref[...] = dnorm
        return
    inv_rms = inv_ref[...]
    normed = saved_ref[...].astype(jnp.float32) * inv_rms
    grad_hat = dnorm * gain_ref[...]
    term = inv_rms * (grad_hat - normed * jnp.mean(grad_hat * normed, axis=-1, keepdims=True))
    term = term.astype(jnp.bfloat16)
    shares, _, share_width = out_ref.shape
    for share in range(shares):
        out_ref[share] = term[:, share * share_width : (share + 1) * share_width]


def run_chunk(mask, gains, low, grad, weight, total, extra, part, parts, shares, head_dim):
    rows, feat = low.shape[0] // parts, low.shape[1]
    width = weight.shape[1] // 4
    block = mask.shape[0]
    tile = 2 * block if rows % (2 * block) == 0 else block
    steps = rows // tile
    first, last = total is None, extra is not None

    def at(step):
        return (part * steps + step, 0)

    def whole(step):
        return (0, 0)

    once = pl.Buffered(1)
    in_specs = [
        pl.BlockSpec(mask.shape, whole, pipeline_mode=once),
        pl.BlockSpec(gains.shape, whole, pipeline_mode=once),
        pl.BlockSpec((tile, feat), at),
        pl.BlockSpec((tile, feat), at),
        pl.BlockSpec(weight.shape, whole, pipeline_mode=once),
    ]
    args = [mask, gains, low, grad, weight]
    if not first:
        in_specs.append(pl.BlockSpec((tile, feat), at))
        args.append(total)
    if last:
        saved, inv_rms, gain_row = extra
        in_specs += [
            pl.BlockSpec((tile, feat), at),
            pl.BlockSpec((tile, 1), at),
            pl.BlockSpec(gain_row.shape, whole, pipeline_mode=once),
        ]
        args += [saved, inv_rms, gain_row]
        share_width = feat // shares
        out_shape = jax.ShapeDtypeStruct((shares, rows, share_width), jnp.bfloat16)
        out_specs = pl.BlockSpec((shares, tile, share_width), lambda step: (0, step, 0))
    else:
        out_shape = jax.ShapeDtypeStruct((rows, feat), jnp.float32)
        out_specs = pl.BlockSpec((tile, feat), lambda step: (step, 0))
    moved = rows * feat * (4 + 4 * (not first) + 4 * (not last)) + weight.size * 2
    return pl.pallas_call(
        functools.partial(chunk_kernel, first, last, width, head_dim, block),
        grid=(steps,),
        in_specs=in_specs,
        out_specs=out_specs,
        out_shape=out_shape,
        scratch_shapes=[pltpu.VMEM((tile, 3 * width), jnp.bfloat16)],
        input_output_aliases={5: 0} if (not first and not last) else {},
        compiler_params=pltpu.CompilerParams(
            dimension_semantics=("arbitrary",), vmem_limit_bytes=48 << 20
        ),
        cost_estimate=pl.CostEstimate(
            flops=14 * rows * feat * width, bytes_accessed=moved, transcendentals=rows * width
        ),
        name="chunk_last" if last else "chunk",
    )(*args)


def on_device(inputs, upstream, norm_gain, head_gain, w_query, w_key, w_value, w_out):
    on_last = lax.axis_index("section") == 1
    frame_count, head_count = lax.axis_size("frame"), lax.axis_size("head")
    my_frame, my_head = lax.axis_index("frame"), lax.axis_index("head")
    batches, frames, patches, feat = inputs.shape[1:]
    rows = frames * patches
    total_frames = frames * frame_count
    few = patches // frame_count
    piece = frames * few
    head_dim = head_gain.shape[-1]
    share = feat // head_count
    local_width = w_query.shape[2]
    width = 2 * head_dim if local_width % (2 * head_dim) == 0 else head_dim
    chunks = local_width // width
    gain_row = norm_gain
    gains = jnp.stack([head_gain[0, 0] * head_dim ** (-0.5), head_gain[0, 1]])

    def reorder(array_in, source):
        pick = (source[:, None] == jnp.arange(rows)[None, :]).astype(jnp.bfloat16)
        flat = array_in.reshape(-1, rows, array_in.shape[-1])
        moved = jnp.einsum("rs,bsc->brc", pick, flat, preferred_element_type=jnp.float32)
        return moved.astype(jnp.bfloat16)

    index = jnp.arange(rows)
    shift, in_frame, in_few = index // piece, (index % piece) // few, index % few
    target = (my_frame + shift) % frame_count
    leave_space = in_frame * patches + target * few + in_few
    leave_time = in_few * total_frames + target * frames + in_frame
    time_patch, time_frame = index // total_frames, index % total_frames
    enter_time = (
        ((my_frame - time_frame // frames) % frame_count) * piece
        + (time_frame % frames) * few
        + time_patch
    )
    space_frame, space_patch = index // patches, index % patches
    enter_space = (
        ((my_frame - space_patch // few) % frame_count) * piece
        + space_frame * few
        + space_patch % few
    )

    def exchange(array_in, leave, enter, from_section):
        sorted_rows = reorder(array_in, leave)
        pieces = []
        for step in range(frame_count):
            part = sorted_rows[:, step * piece : (step + 1) * piece]
            if step or from_section:
                part = lax.ppermute(
                    part,
                    ("section", "frame"),
                    [
                        (from_section * frame_count + source, (source + step) % frame_count)
                        for source in range(frame_count)
                    ],
                )
            pieces.append(part)
        return reorder(jnp.concatenate(pieces, axis=1), enter)

    def swap(array_in, bit):
        return lax.ppermute(array_in, "head", [(i, i ^ bit) for i in range(head_count)])

    my_core, my_side = my_head % 2, my_head // 2

    def gather_share(own):
        far = swap(own, 2)
        low_side = jnp.where(my_side == 0, own, far)
        high_side = jnp.where(my_side == 0, far, own)
        both = jnp.stack([low_side, high_side])
        other = swap(both, 1)
        first, second = jnp.where(my_core == 0, both, other), jnp.where(my_core == 0, other, both)
        return jnp.concatenate([first[0], second[0], first[1], second[1]], axis=-1)

    def sum_share(term):
        shaped = term.reshape(2, 2, *term.shape[1:])
        keep = lax.dynamic_index_in_dim(shaped, my_core, 1, keepdims=False)
        other = swap(lax.dynamic_index_in_dim(shaped, 1 - my_core, 1, keepdims=False), 1)
        pair = keep.astype(jnp.float32) + other.astype(jnp.float32)
        far = lax.dynamic_index_in_dim(pair, 1 - my_side, 0, keepdims=False).astype(jnp.bfloat16)
        own = lax.dynamic_index_in_dim(pair, my_side, 0, keepdims=False)
        return own + swap(far, 2).astype(jnp.float32)

    def my_share(array_in):
        return lax.dynamic_slice_in_dim(array_in, my_head * share, share, array_in.ndim - 1)

    def pack(chunk):
        cols = slice(chunk * width, (chunk + 1) * width)
        return jnp.concatenate(
            [w_query[0][:, cols], w_key[0][:, cols], w_value[0][:, cols], w_out[0][cols].T], axis=1
        )

    weights = [lax.all_gather(pack(c), "frame", axis=0, tiled=True) for c in range(chunks)]

    saved_space = inputs[0].reshape(batches, rows, feat)
    saved_time = gather_share(exchange(my_share(saved_space), leave_space, enter_time, 0))
    saved = jnp.where(on_last, saved_space, saved_time).reshape(batches * rows, feat)
    wide = saved.astype(jnp.float32)
    inv_rms = lax.rsqrt(jnp.mean(wide * wide, axis=-1, keepdims=True) + EPS)
    low = (wide * inv_rms * gain_row).astype(jnp.bfloat16)

    place = jnp.arange(patches) // FRAMES
    mask = jnp.where(on_last, 1.0, (place[:, None] == place[None, :]).astype(jnp.float32))
    extra = (saved, inv_rms, gain_row)

    def sublayer(grad, lows, extras):
        total = None
        parts = grad.shape[0] // rows
        for chunk in range(chunks):
            last = chunk == chunks - 1
            if not last:
                total = run_chunk(
                    mask, gains, lows, grad, weights[chunk], total, None, 0, 1, head_count, head_dim
                )
        return [
            run_chunk(
                mask, gains, lows, grad, weights[-1], total, extras, b, parts, head_count, head_dim
            )
            for b in range(parts)
        ]

    grad_space = upstream.reshape(batches * rows, feat)
    share_space = my_share(upstream.reshape(batches, rows, feat))
    space_parts, time_parts = [], []
    for b, term in enumerate(sublayer(grad_space, low, extra)):
        summed = sum_share(term)
        space_parts.append((share_space[b].astype(jnp.float32) + summed).astype(jnp.bfloat16))
    for b in range(batches):
        grad_share = exchange(space_parts[b], leave_space, enter_time, 1)[0]
        grad_time = gather_share(grad_share)
        part = slice(b * rows, (b + 1) * rows)
        (term,) = sublayer(grad_time, low[part], (saved[part], inv_rms[part], gain_row))
        summed = sum_share(term)
        result = (grad_share.astype(jnp.float32) + summed).astype(jnp.bfloat16)
        time_parts.append(exchange(result, leave_time, enter_space, 0)[0])
    result = jnp.where(on_last, jnp.stack(space_parts), jnp.stack(time_parts))
    return result.reshape(1, batches, frames, patches, share)


def solution(mesh):
    in_specs = (
        P("section", None, "frame", None, None),
        P(None, "frame", None, None),
        P("section", None),
        P("section", None, None),
        P("section", "frame", "head"),
        P("section", "frame", "head"),
        P("section", "frame", "head"),
        P("section", "head", "frame"),
    )
    out_specs = P("section", None, "frame", None, "head")
    return jax.shard_map(
        on_device, mesh=mesh, in_specs=in_specs, out_specs=out_specs, check_vma=False
    )
```

```python
import functools

import jax
import jax.numpy as jnp
from jax import lax
from jax.experimental import pallas as pl
from jax.experimental.pallas import tpu as pltpu
from jax.sharding import PartitionSpec as P

FRAMES = 16
EPS = 1e-06


def dot_nn(left, right):
    return lax.dot_general(left, right, (((1,), (0,)), ((), ())), preferred_element_type=jnp.float32)


def dot_nt(left, right):
    return lax.dot_general(left, right, (((1,), (1,)), ((), ())), preferred_element_type=jnp.float32)


def dot_tn(left, right):
    return lax.dot_general(left, right, (((0,), (0,)), ((), ())), preferred_element_type=jnp.float32)


def head_norm(raw_rows):
    scale_rows = lax.rsqrt(jnp.mean(raw_rows * raw_rows, axis=-1, keepdims=True) + EPS)
    return raw_rows * scale_rows, scale_rows


def norm_back(grad_low, normal_hat, scale_rows, gain_vec):
    grad_hat = grad_low.astype(jnp.float32) * gain_vec
    inner_mean = jnp.mean(grad_hat * normal_hat, axis=-1, keepdims=True)
    return (scale_rows * (grad_hat - normal_hat * inner_mean)).astype(jnp.bfloat16)


def attend_back(units, mask):
    scores = [dot_nt(key, query) for query, key, _, _ in units]
    dprobs = [dot_nt(value, grad) for _, _, value, grad in units]
    expo = [jnp.exp(score) * mask for score in scores]
    probs = [x * (1.0 / jnp.sum(x, axis=0, keepdims=True)) for x in expo]
    inner = [jnp.sum(p * d, axis=0, keepdims=True) for p, d in zip(probs, dprobs)]
    dscores = [(p * (d - i)).astype(jnp.bfloat16) for p, d, i in zip(probs, dprobs, inner)]
    dvalues = [dot_nn(p.astype(jnp.bfloat16), unit[3]) for p, unit in zip(probs, units)]
    dkeys = [dot_nn(d, unit[0]) for d, unit in zip(dscores, units)]
    dqueries = [dot_tn(d, unit[1]) for d, unit in zip(dscores, units)]
    return [
        tuple(x.astype(jnp.bfloat16) for x in triple) for triple in zip(dqueries, dkeys, dvalues)
    ]


def raw_kernel(source_ref, low_ref, *refs):
    *piece_refs, raw_ref = refs
    total = None
    for slot, piece_ref in enumerate(piece_refs):
        depth = piece_ref.shape[0]
        start = pl.multiple_of(source_ref[slot] * depth, depth)
        part = dot_nn(low_ref[:, pl.ds(start, depth)], piece_ref[...])
        total = part if total is None else total + part
    raw_ref[...] = total


def run_raw(sources, low, pieces):
    rows, feat = low.shape
    columns = pieces[0].shape[1]
    tile = rows // 4
    once = pl.Buffered(1)
    return pl.pallas_call(
        raw_kernel,
        grid_spec=pltpu.PrefetchScalarGridSpec(
            num_scalar_prefetch=1,
            grid=(rows // tile,),
            in_specs=[pl.BlockSpec((tile, feat), lambda i, source: (i, 0))]
            + [
                pl.BlockSpec(piece.shape, lambda i, source: (0, 0), pipeline_mode=once)
                for piece in pieces
            ],
            out_specs=pl.BlockSpec((tile, columns), lambda i, source: (i, 0)),
        ),
        out_shape=jax.ShapeDtypeStruct((rows, columns), jnp.float32),
        compiler_params=pltpu.CompilerParams(
            dimension_semantics=("arbitrary",), vmem_limit_bytes=40 << 20
        ),
        cost_estimate=pl.CostEstimate(
            flops=2 * rows * feat * columns,
            bytes_accessed=2 * feat * columns + 2 * rows * feat + 4 * rows * columns,
            transcendentals=0,
        ),
        name="raw_products",
    )(sources, low, *pieces)


def back_kernel(chunks, slots, head_dim, first_grad, first_saved, flag_ref, source_ref, *refs):
    @pl.when(flag_ref[0] == 1)
    def _():
        back_body(chunks, slots, head_dim, first_grad, first_saved, source_ref, *refs)


def back_body(chunks, slots, head_dim, first_grad, first_saved, source_ref, *refs):
    (mask_ref, gains_ref, inv_ref, gain_ref, grad_hbm, saved_hbm), refs = refs[:6], refs[6:]
    raw_hbm, refs = refs[:chunks], refs[chunks:]
    out_weight_hbm, refs = refs[:slots], refs[slots:]
    weight_hbm, refs = refs[: chunks * slots], refs[chunks * slots :]
    term_hbm, grad_ref, saved_ref, raw_ref, out_weight_ref, weight_ref = refs[:6]
    total_ref, packed_ref, term_ref, arrived = refs[6:]
    rows, feat = grad_ref.shape
    block = mask_ref.shape[0]
    depth, columns = weight_hbm[0].shape
    width = columns // 3
    places = [pl.multiple_of(source_ref[slot] * depth, depth) for slot in range(slots)]
    started = [0]

    def start(source, target):
        copy = pltpu.make_async_copy(source, target, arrived.at[started[0]])
        started[0] += 1
        copy.start()
        return copy

    get_first = [start(grad_hbm.at[pl.ds(first_grad, rows)], grad_ref)]
    for slot in range(slots):
        target = out_weight_ref.at[:, pl.ds(places[slot], depth)]
        get_first.append(start(out_weight_hbm[slot], target))
    get_raw = [
        start(raw_hbm[chunk].at[pl.ds(first_saved, rows)], raw_ref.at[chunk])
        for chunk in range(chunks)
    ]
    for copy in get_first:
        copy.wait()
    get_rest = []
    for slot in range(slots):
        for chunk in range(chunks):
            target = weight_ref.at[pl.ds(places[slot], depth), pl.ds(chunk * columns, columns)]
            get_rest.append(start(weight_hbm[chunk * slots + slot], target))
    get_rest.append(start(saved_hbm.at[pl.ds(first_saved, rows)], saved_ref))

    query_gain, key_gain = gains_ref[0:1, :], gains_ref[1:2, :]
    mask = mask_ref[...]
    grad_attn = dot_nt(grad_ref[...], out_weight_ref[...]).astype(jnp.bfloat16)
    for chunk in range(chunks):
        get_raw[chunk].wait()
        for head in range(width // head_dim):
            query_cols = slice(head * head_dim, (head + 1) * head_dim)
            key_cols = slice(width + query_cols.start, width + query_cols.stop)
            value_cols = slice(2 * width + query_cols.start, 2 * width + query_cols.stop)
            grad_cols = slice(chunk * width + query_cols.start, chunk * width + query_cols.stop)

            def out_cols(cols):
                return slice(chunk * columns + cols.start, chunk * columns + cols.stop)

            for begin in range(0, rows, 4 * block):
                owns = [
                    slice(first, first + block)
                    for first in range(begin, min(rows, begin + 4 * block), block)
                ]
                queries = [head_norm(raw_ref[chunk, own, query_cols]) for own in owns]
                keys = [head_norm(raw_ref[chunk, own, key_cols]) for own in owns]
                units = [
                    (
                        (query[0] * query_gain).astype(jnp.bfloat16),
                        (key[0] * key_gain).astype(jnp.bfloat16),
                        raw_ref[chunk, own, value_cols].astype(jnp.bfloat16),
                        grad_attn[own, grad_cols],
                    )
                    for own, query, key in zip(owns, queries, keys)
                ]
                backs = attend_back(units, mask)
                for own, query, key, (dquery, dkey, dvalue) in zip(owns, queries, keys, backs):
                    packed_ref[own, out_cols(query_cols)] = norm_back(dquery, *query, query_gain)
                    packed_ref[own, out_cols(key_cols)] = norm_back(dkey, *key, key_gain)
                    packed_ref[own, out_cols(value_cols)] = dvalue
    for copy in get_rest:
        copy.wait()
    shares, _, share_width = term_ref.shape
    packed = packed_ref[...]
    for share in range(shares):
        part = slice(share * share_width, (share + 1) * share_width)
        total_ref[:, part] = dot_nt(packed, weight_ref[part, :])
    sends = []
    for first in range(0, rows, block):
        own = slice(first, first + block)
        inv_rms = inv_ref[first_saved + first : first_saved + first + block, :]
        normed = saved_ref[own, :].astype(jnp.float32) * inv_rms
        grad_hat = total_ref[own, :] * gain_ref[...]
        inner_mean = jnp.mean(grad_hat * normed, axis=-1, keepdims=True)
        term = (inv_rms * (grad_hat - normed * inner_mean)).astype(jnp.bfloat16)
        for share in range(shares):
            term_ref[share, own, :] = term[:, share * share_width : (share + 1) * share_width]
        window = pl.ds(first, block)
        sends.append(start(term_ref.at[:, window], term_hbm.at[:, window]))
    for send in sends:
        send.wait()


def run_back(flag, sources, mask, gains, inv_rms, gain_row, grad, first_grad, saved, first_saved, rows, raws, out_pieces, pieces, shares, head_dim):
    feat = grad.shape[1]
    chunks, slots = len(raws), len(out_pieces)
    columns = pieces[0][0].shape[1]
    heads_width = out_pieces[0].shape[0]
    share_width = feat // shares
    block = mask.shape[0]
    vmem = pl.BlockSpec(memory_space=pltpu.VMEM)
    smem = pl.BlockSpec(memory_space=pltpu.SMEM)
    anywhere = pl.BlockSpec(memory_space=pl.ANY)
    arrays = [grad, saved, *raws, *out_pieces, *(piece for group in pieces for piece in group)]
    copies = len(arrays) + rows // block
    return pl.pallas_call(
        functools.partial(back_kernel, chunks, slots, head_dim, first_grad, first_saved),
        in_specs=[smem] * 2 + [vmem] * 4 + [anywhere] * len(arrays),
        out_specs=anywhere,
        out_shape=jax.ShapeDtypeStruct((shares, rows, share_width), jnp.bfloat16),
        scratch_shapes=[
            pltpu.VMEM((rows, feat), jnp.bfloat16),
            pltpu.VMEM((rows, feat), jnp.bfloat16),
            pltpu.VMEM((chunks, rows, columns), jnp.float32),
            pltpu.VMEM((heads_width, feat), jnp.bfloat16),
            pltpu.VMEM((feat, chunks * columns), jnp.bfloat16),
            pltpu.VMEM((rows, feat), jnp.float32),
            pltpu.VMEM((rows, chunks * columns), jnp.bfloat16),
            pltpu.VMEM((shares, rows, share_width), jnp.bfloat16),
            pltpu.SemaphoreType.DMA((copies,)),
        ],
        compiler_params=pltpu.CompilerParams(vmem_limit_bytes=56 << 20),
        cost_estimate=pl.CostEstimate(
            flops=16 * rows * feat * heads_width,
            bytes_accessed=8 * feat * heads_width + 6 * rows * feat,
            transcendentals=rows * heads_width,
        ),
        name="sublayer_back",
    )(flag, sources, mask, gains, inv_rms, gain_row, *arrays)


def on_device(inputs, upstream, norm_gain, head_gain, w_query, w_key, w_value, w_out):
    on_last = lax.axis_index("section") == 1
    frame_count, head_count = lax.axis_size("frame"), lax.axis_size("head")
    my_frame, my_head = lax.axis_index("frame"), lax.axis_index("head")
    batches, frames, patches, feat = inputs.shape[1:]
    rows = frames * patches
    total_frames = frames * frame_count
    few = patches // frame_count
    piece = frames * few
    head_dim = head_gain.shape[-1]
    share = feat // head_count
    local_width = w_query.shape[2]
    width = 2 * head_dim if local_width % (2 * head_dim) == 0 else head_dim
    chunks = local_width // width
    gain_row = norm_gain
    gains = jnp.stack([head_gain[0, 0] * head_dim ** (-0.5), head_gain[0, 1]])

    def reorder(array_in, source):
        pick = (source[:, None] == jnp.arange(rows)[None, :]).astype(jnp.bfloat16)
        flat = array_in.reshape(-1, rows, array_in.shape[-1])
        moved = jnp.einsum("rs,bsc->brc", pick, flat, preferred_element_type=jnp.float32)
        return moved.astype(jnp.bfloat16)

    index = jnp.arange(rows)
    shift, in_frame, in_few = index // piece, (index % piece) // few, index % few
    target = (my_frame + shift) % frame_count
    leave_space = in_frame * patches + target * few + in_few
    leave_time = in_few * total_frames + target * frames + in_frame
    time_patch, time_frame = index // total_frames, index % total_frames
    enter_time = (
        ((my_frame - time_frame // frames) % frame_count) * piece
        + (time_frame % frames) * few
        + time_patch
    )
    space_frame, space_patch = index // patches, index % patches
    enter_space = (
        ((my_frame - space_patch // few) % frame_count) * piece
        + space_frame * few
        + space_patch % few
    )

    def send_rows(array_in, leave, from_section):
        sorted_rows = reorder(array_in, leave)
        parts = []
        for step in range(frame_count):
            part = sorted_rows[:, step * piece : (step + 1) * piece]
            if step or from_section:
                part = lax.ppermute(
                    part,
                    ("section", "frame"),
                    [
                        (from_section * frame_count + source, (source + step) % frame_count)
                        for source in range(frame_count)
                    ],
                )
            parts.append(part)
        return parts

    def place_rows(parts, enter):
        return reorder(jnp.concatenate(parts, axis=1), enter)

    def swap(array_in, bit):
        return lax.ppermute(array_in, "head", [(i, i ^ bit) for i in range(head_count)])

    my_core, my_side = my_head % 2, my_head // 2

    def gather_share(own):
        far = swap(own, 2)
        low_side = jnp.where(my_side == 0, own, far)
        high_side = jnp.where(my_side == 0, far, own)
        both = jnp.stack([low_side, high_side])
        other = swap(both, 1)
        first, second = jnp.where(my_core == 0, both, other), jnp.where(my_core == 0, other, both)
        return jnp.concatenate([first[0], second[0], first[1], second[1]], axis=-1)

    def core_sum(term):
        shaped = term.reshape(2, 2, *term.shape[1:])
        keep = lax.dynamic_index_in_dim(shaped, my_core, 1, keepdims=False)
        other = swap(lax.dynamic_index_in_dim(shaped, 1 - my_core, 1, keepdims=False), 1)
        pair = keep.astype(jnp.float32) + other.astype(jnp.float32)
        far = lax.dynamic_index_in_dim(pair, 1 - my_side, 0, keepdims=False).astype(jnp.bfloat16)
        return lax.dynamic_index_in_dim(pair, my_side, 0, keepdims=False), far

    def side_sum(own, far):
        return own + swap(far, 2).astype(jnp.float32)

    def my_share(array_in):
        return lax.dynamic_slice_in_dim(array_in, my_head * share, share, array_in.ndim - 1)

    def along(array_in, pairs):
        return lax.ppermute(array_in, "frame", pairs)

    at_end = jnp.logical_or(my_frame == 0, my_frame == 3)
    outer, inner = [(0, 1), (1, 0), (2, 3), (3, 2)], [(1, 2), (2, 1)]

    def fetch(shards):
        near = [along(x, outer) for x in shards]
        middle = [along(x, inner) for x in shards]
        across = [along(x, inner) for x in near]
        second = [jnp.where(at_end, along(x, outer), x) for x in middle]
        return near, second, across

    def last_hop(across):
        return jnp.where(at_end, along(across, outer), across)

    if frame_count == 4:
        upper = my_frame // 2
        sources = jnp.stack([my_frame, my_frame + 1 - 2 * (my_frame % 2), 2 - upper, 3 - 3 * upper])
    else:
        sources = jnp.zeros((1,), jnp.int32)
    sources = sources.astype(jnp.int32)

    shards = []
    for chunk in range(chunks):
        cols = slice(chunk * width, (chunk + 1) * width)
        columns = [w_query[0][:, cols], w_key[0][:, cols], w_value[0][:, cols]]
        shards.append(jnp.concatenate(columns, axis=1))
    shards.append(w_out[0])

    saved_space = inputs[0].reshape(batches, rows, feat)
    share_saved = my_share(saved_space)
    if frame_count == 4:
        near, second, across = fetch(shards)
    saved_time = gather_share(place_rows(send_rows(share_saved, leave_space, 0), enter_time))
    saved = jnp.where(on_last, saved_space, saved_time).reshape(batches * rows, feat)
    wide = saved.astype(jnp.float32)
    inv_rms = lax.rsqrt(jnp.mean(wide * wide, axis=-1, keepdims=True) + EPS)
    low = (wide * inv_rms * gain_row).astype(jnp.bfloat16)

    place = jnp.arange(patches) // FRAMES
    mask = jnp.where(on_last, 1.0, (place[:, None] == place[None, :]).astype(jnp.float32))
    raws, pieces = [], []
    if frame_count == 4:
        for chunk in range(chunks):
            pieces.append([shards[chunk], near[chunk], second[chunk], last_hop(across[chunk])])
            raws.append(run_raw(sources, low, pieces[-1]))
        *_, across[-1] = lax.optimization_barrier((*raws[:-1], across[-1]))
        out_pieces = [shards[-1], near[-1], second[-1], last_hop(across[-1])]
    else:
        for chunk in range(chunks):
            pieces.append([lax.all_gather(shards[chunk], "frame", axis=0, tiled=True)])
            raws.append(run_raw(sources, low, pieces[-1]))
        out_pieces = [lax.all_gather(shards[-1], "frame", axis=1, tiled=True)]
    flags = [(lax.axis_index("section") == s).astype(jnp.int32).reshape(1) for s in range(2)]
    halves = 2 if rows % (2 * patches) == 0 else 1

    def sublayer(flag, grad, first_grad, first, count):
        return run_back(
            flag, sources, mask, gains, inv_rms, gain_row, grad, first_grad, saved, first, count,
            raws, out_pieces, pieces, head_count, head_dim,
        )

    def in_parts(flag, grad, first_grad, b, count, tie=None):
        sums, first_term = [], None
        for start in range(0, rows, count):
            if tie is not None and start + count == rows:
                flag, tie = lax.optimization_barrier((flag, tie))
            term = sublayer(flag, grad, first_grad + start, b * rows + start, count)
            first_term = term if first_term is None else first_term
            sums.append(side_sum(*core_sum(term)))
        return jnp.concatenate(sums, axis=0), first_term, tie

    def add(residual, summed):
        return (residual.astype(jnp.float32) + summed).astype(jnp.bfloat16)

    grad_space = upstream.reshape(batches * rows, feat)
    share_space = my_share(upstream.reshape(batches, rows, feat))
    space_parts, sent, shares, fulls = [], [], [], []

    def receive(arrived):
        shares.append(place_rows(arrived, enter_time)[0])
        fulls.append(gather_share(shares[-1]))

    for b in range(batches):
        tie = space_parts[-1] if b else None
        count = rows // halves if b else rows
        summed, _, tie = in_parts(flags[1], grad_space, b * rows, b, count, tie)
        if b:
            space_parts[-1] = tie
            receive(send_rows(tie, leave_space, 1))
            summed, fulls[-1] = lax.optimization_barrier((summed, fulls[-1]))
        space_parts.append(add(share_space[b], summed))
    sent = send_rows(space_parts[-1], leave_space, 1)
    time_parts, returned, first_term = [], [], None
    for b in range(batches):
        if b == batches - 1:
            if b:
                sent, first_term = lax.optimization_barrier((sent, first_term))
            receive(sent)
        tie = time_parts[-1] if b else None
        summed, first_term, tie = in_parts(flags[0], fulls[b], 0, b, rows // halves, tie)
        if b:
            time_parts[-1] = tie
            returned.append(send_rows(tie, leave_time, 0))
        time_parts.append(add(shares[b], summed))
    returned.append(send_rows(time_parts[-1], leave_time, 0))
    time_parts = [place_rows(parts, enter_space)[0] for parts in returned]
    result = jnp.where(on_last, jnp.stack(space_parts), jnp.stack(time_parts))
    return result.reshape(1, batches, frames, patches, share)


def solution(mesh):
    in_specs = (
        P("section", None, "frame", None, None),
        P(None, "frame", None, None),
        P("section", None),
        P("section", None, None),
        P("section", "frame", "head"),
        P("section", "frame", "head"),
        P("section", "frame", "head"),
        P("section", "head", "frame"),
    )
    out_specs = P("section", None, "frame", None, "head")
    return jax.shard_map(
        on_device, mesh=mesh, in_specs=in_specs, out_specs=out_specs, check_vma=False
    )
```

```python
import functools

import jax
import jax.numpy as jnp
from jax import lax
from jax.experimental import pallas as pl
from jax.experimental.pallas import tpu as pltpu
from jax.sharding import PartitionSpec as P

FRAMES = 16
EPS = 1e-06


def dot_nn(left, right):
    return lax.dot_general(left, right, (((1,), (0,)), ((), ())), preferred_element_type=jnp.float32)


def dot_nt(left, right):
    return lax.dot_general(left, right, (((1,), (1,)), ((), ())), preferred_element_type=jnp.float32)


def dot_tn(left, right):
    return lax.dot_general(left, right, (((0,), (0,)), ((), ())), preferred_element_type=jnp.float32)


def head_norm(raw_rows):
    scale_rows = lax.rsqrt(jnp.mean(raw_rows * raw_rows, axis=-1, keepdims=True) + EPS)
    return raw_rows * scale_rows, scale_rows


def norm_back(grad_low, normal_hat, scale_rows, gain_vec):
    grad_hat = grad_low.astype(jnp.float32) * gain_vec
    inner_mean = jnp.mean(grad_hat * normal_hat, axis=-1, keepdims=True)
    return (scale_rows * (grad_hat - normal_hat * inner_mean)).astype(jnp.bfloat16)


def attend_back(units, mask):
    scores = [dot_nt(key, query) for query, key, _, _ in units]
    dprobs = [dot_nt(value, grad) for _, _, value, grad in units]
    expo = [jnp.exp(score) * mask for score in scores]
    probs = [x * (1.0 / jnp.sum(x, axis=0, keepdims=True)) for x in expo]
    inner = [jnp.sum(p * d, axis=0, keepdims=True) for p, d in zip(probs, dprobs)]
    dscores = [(p * (d - i)).astype(jnp.bfloat16) for p, d, i in zip(probs, dprobs, inner)]
    dvalues = [dot_nn(p.astype(jnp.bfloat16), unit[3]) for p, unit in zip(probs, units)]
    dkeys = [dot_nn(d, unit[0]) for d, unit in zip(dscores, units)]
    dqueries = [dot_tn(d, unit[1]) for d, unit in zip(dscores, units)]
    return [
        tuple(x.astype(jnp.bfloat16) for x in triple) for triple in zip(dqueries, dkeys, dvalues)
    ]


def raw_kernel(source_ref, low_ref, *refs):
    *piece_refs, raw_ref = refs
    total = None
    for slot, piece_ref in enumerate(piece_refs):
        depth = piece_ref.shape[0]
        start = pl.multiple_of(source_ref[slot] * depth, depth)
        part = dot_nn(low_ref[:, pl.ds(start, depth)], piece_ref[...])
        total = part if total is None else total + part
    raw_ref[...] = total


def run_raw(sources, low, pieces):
    rows, feat = low.shape
    columns = pieces[0].shape[1]
    tile = rows // 4
    once = pl.Buffered(1)
    return pl.pallas_call(
        raw_kernel,
        grid_spec=pltpu.PrefetchScalarGridSpec(
            num_scalar_prefetch=1,
            grid=(rows // tile,),
            in_specs=[pl.BlockSpec((tile, feat), lambda i, source: (i, 0))]
            + [
                pl.BlockSpec(piece.shape, lambda i, source: (0, 0), pipeline_mode=once)
                for piece in pieces
            ],
            out_specs=pl.BlockSpec((tile, columns), lambda i, source: (i, 0)),
        ),
        out_shape=jax.ShapeDtypeStruct((rows, columns), jnp.float32),
        compiler_params=pltpu.CompilerParams(
            dimension_semantics=("arbitrary",), vmem_limit_bytes=40 << 20
        ),
        cost_estimate=pl.CostEstimate(
            flops=2 * rows * feat * columns,
            bytes_accessed=2 * feat * columns + 2 * rows * feat + 4 * rows * columns,
            transcendentals=0,
        ),
        name="raw_products",
    )(sources, low, *pieces)


def back_kernel(chunks, slots, head_dim, first_grad, first_saved, flag_ref, source_ref, *refs):
    @pl.when(flag_ref[0] == 1)
    def _():
        back_body(chunks, slots, head_dim, first_grad, first_saved, source_ref, *refs)


def back_body(chunks, slots, head_dim, first_grad, first_saved, source_ref, *refs):
    (mask_ref, gains_ref, inv_ref, gain_ref, grad_hbm, saved_hbm), refs = refs[:6], refs[6:]
    raw_hbm, refs = refs[:chunks], refs[chunks:]
    out_weight_hbm, refs = refs[:slots], refs[slots:]
    weight_hbm, refs = refs[: chunks * slots], refs[chunks * slots :]
    term_hbm, grad_ref, saved_ref, raw_ref, out_weight_ref, weight_ref = refs[:6]
    total_ref, packed_ref, term_ref, arrived = refs[6:]
    rows, feat = grad_ref.shape
    block = mask_ref.shape[0]
    depth, columns = weight_hbm[0].shape
    width = columns // 3
    places = [pl.multiple_of(source_ref[slot] * depth, depth) for slot in range(slots)]
    started = [0]

    def start(source, target):
        copy = pltpu.make_async_copy(source, target, arrived.at[started[0]])
        started[0] += 1
        copy.start()
        return copy

    get_first = [start(grad_hbm.at[pl.ds(first_grad, rows)], grad_ref)]
    for slot in range(slots):
        target = out_weight_ref.at[:, pl.ds(places[slot], depth)]
        get_first.append(start(out_weight_hbm[slot], target))
    for copy in get_first:
        copy.wait()
    get_raw = [
        start(raw_hbm[chunk].at[pl.ds(first_saved, rows)], raw_ref.at[chunk])
        for chunk in range(chunks)
    ]
    get_rest = []
    for slot in range(slots):
        for chunk in range(chunks):
            target = weight_ref.at[pl.ds(places[slot], depth), pl.ds(chunk * columns, columns)]
            get_rest.append(start(weight_hbm[chunk * slots + slot], target))
    get_rest.append(start(saved_hbm.at[pl.ds(first_saved, rows)], saved_ref))

    query_gain, key_gain = gains_ref[0:1, :], gains_ref[1:2, :]
    mask = mask_ref[...]
    grad_attn = dot_nt(grad_ref[...], out_weight_ref[...]).astype(jnp.bfloat16)
    for chunk in range(chunks):
        get_raw[chunk].wait()
        for head in range(width // head_dim):
            query_cols = slice(head * head_dim, (head + 1) * head_dim)
            key_cols = slice(width + query_cols.start, width + query_cols.stop)
            value_cols = slice(2 * width + query_cols.start, 2 * width + query_cols.stop)
            grad_cols = slice(chunk * width + query_cols.start, chunk * width + query_cols.stop)

            def out_cols(cols):
                return slice(chunk * columns + cols.start, chunk * columns + cols.stop)

            for begin in range(0, rows, 4 * block):
                owns = [
                    slice(first, first + block)
                    for first in range(begin, min(rows, begin + 4 * block), block)
                ]
                queries = [head_norm(raw_ref[chunk, own, query_cols]) for own in owns]
                keys = [head_norm(raw_ref[chunk, own, key_cols]) for own in owns]
                units = [
                    (
                        (query[0] * query_gain).astype(jnp.bfloat16),
                        (key[0] * key_gain).astype(jnp.bfloat16),
                        raw_ref[chunk, own, value_cols].astype(jnp.bfloat16),
                        grad_attn[own, grad_cols],
                    )
                    for own, query, key in zip(owns, queries, keys)
                ]
                backs = attend_back(units, mask)
                for own, query, key, (dquery, dkey, dvalue) in zip(owns, queries, keys, backs):
                    packed_ref[own, out_cols(query_cols)] = norm_back(dquery, *query, query_gain)
                    packed_ref[own, out_cols(key_cols)] = norm_back(dkey, *key, key_gain)
                    packed_ref[own, out_cols(value_cols)] = dvalue
    for copy in get_rest:
        copy.wait()
    shares, _, share_width = term_ref.shape
    packed = packed_ref[...]
    for share in range(shares):
        part = slice(share * share_width, (share + 1) * share_width)
        total_ref[:, part] = dot_nt(packed, weight_ref[part, :])
    sends = []
    for first in range(0, rows, block):
        own = slice(first, first + block)
        inv_rms = inv_ref[first_saved + first : first_saved + first + block, :]
        normed = saved_ref[own, :].astype(jnp.float32) * inv_rms
        grad_hat = total_ref[own, :] * gain_ref[...]
        inner_mean = jnp.mean(grad_hat * normed, axis=-1, keepdims=True)
        term = (inv_rms * (grad_hat - normed * inner_mean)).astype(jnp.bfloat16)
        for share in range(shares):
            term_ref[share, own, :] = term[:, share * share_width : (share + 1) * share_width]
        window = pl.ds(first, block)
        sends.append(start(term_ref.at[:, window], term_hbm.at[:, window]))
    for send in sends:
        send.wait()


def run_back(flag, sources, mask, gains, inv_rms, gain_row, grad, first_grad, saved, first_saved, rows, raws, out_pieces, pieces, shares, head_dim):
    feat = grad.shape[1]
    chunks, slots = len(raws), len(out_pieces)
    columns = pieces[0][0].shape[1]
    heads_width = out_pieces[0].shape[0]
    share_width = feat // shares
    block = mask.shape[0]
    vmem = pl.BlockSpec(memory_space=pltpu.VMEM)
    smem = pl.BlockSpec(memory_space=pltpu.SMEM)
    anywhere = pl.BlockSpec(memory_space=pl.ANY)
    arrays = [grad, saved, *raws, *out_pieces, *(piece for group in pieces for piece in group)]
    copies = len(arrays) + rows // block
    return pl.pallas_call(
        functools.partial(back_kernel, chunks, slots, head_dim, first_grad, first_saved),
        in_specs=[smem] * 2 + [vmem] * 4 + [anywhere] * len(arrays),
        out_specs=anywhere,
        out_shape=jax.ShapeDtypeStruct((shares, rows, share_width), jnp.bfloat16),
        scratch_shapes=[
            pltpu.VMEM((rows, feat), jnp.bfloat16),
            pltpu.VMEM((rows, feat), jnp.bfloat16),
            pltpu.VMEM((chunks, rows, columns), jnp.float32),
            pltpu.VMEM((heads_width, feat), jnp.bfloat16),
            pltpu.VMEM((feat, chunks * columns), jnp.bfloat16),
            pltpu.VMEM((rows, feat), jnp.float32),
            pltpu.VMEM((rows, chunks * columns), jnp.bfloat16),
            pltpu.VMEM((shares, rows, share_width), jnp.bfloat16),
            pltpu.SemaphoreType.DMA((copies,)),
        ],
        compiler_params=pltpu.CompilerParams(vmem_limit_bytes=56 << 20),
        cost_estimate=pl.CostEstimate(
            flops=16 * rows * feat * heads_width,
            bytes_accessed=8 * feat * heads_width + 6 * rows * feat,
            transcendentals=rows * heads_width,
        ),
        name="sublayer_back",
    )(flag, sources, mask, gains, inv_rms, gain_row, *arrays)


def on_device(inputs, upstream, norm_gain, head_gain, w_query, w_key, w_value, w_out):
    on_last = lax.axis_index("section") == 1
    frame_count, head_count = lax.axis_size("frame"), lax.axis_size("head")
    my_frame, my_head = lax.axis_index("frame"), lax.axis_index("head")
    batches, frames, patches, feat = inputs.shape[1:]
    rows = frames * patches
    total_frames = frames * frame_count
    few = patches // frame_count
    piece = frames * few
    head_dim = head_gain.shape[-1]
    share = feat // head_count
    local_width = w_query.shape[2]
    width = 2 * head_dim if local_width % (2 * head_dim) == 0 else head_dim
    chunks = local_width // width
    gain_row = norm_gain
    gains = jnp.stack([head_gain[0, 0] * head_dim ** (-0.5), head_gain[0, 1]])

    def reorder(array_in, source):
        pick = (source[:, None] == jnp.arange(rows)[None, :]).astype(jnp.bfloat16)
        flat = array_in.reshape(-1, rows, array_in.shape[-1])
        moved = jnp.einsum("rs,bsc->brc", pick, flat, preferred_element_type=jnp.float32)
        return moved.astype(jnp.bfloat16)

    index = jnp.arange(rows)
    shift, in_frame, in_few = index // piece, (index % piece) // few, index % few
    target = (my_frame + shift) % frame_count
    leave_space = in_frame * patches + target * few + in_few
    leave_time = in_few * total_frames + target * frames + in_frame
    time_patch, time_frame = index // total_frames, index % total_frames
    enter_time = (
        ((my_frame - time_frame // frames) % frame_count) * piece
        + (time_frame % frames) * few
        + time_patch
    )
    space_frame, space_patch = index // patches, index % patches
    enter_space = (
        ((my_frame - space_patch // few) % frame_count) * piece
        + space_frame * few
        + space_patch % few
    )

    def send_rows(array_in, leave, from_section):
        sorted_rows = reorder(array_in, leave)
        parts = []
        for step in range(frame_count):
            part = sorted_rows[:, step * piece : (step + 1) * piece]
            if step or from_section:
                part = lax.ppermute(
                    part,
                    ("section", "frame"),
                    [
                        (from_section * frame_count + source, (source + step) % frame_count)
                        for source in range(frame_count)
                    ],
                )
            parts.append(part)
        return parts

    def place_rows(parts, enter):
        return reorder(jnp.concatenate(parts, axis=1), enter)

    def swap(array_in, bit, section):
        first = section * head_count
        pairs = [(first + i, first + (i ^ bit)) for i in range(head_count)]
        return lax.ppermute(array_in, ("section", "head"), pairs)

    my_core, my_side = my_head % 2, my_head // 2

    def gather_share(own, tie=None):
        far = swap(own, 2, 0)
        if tie is not None:
            far, _ = lax.optimization_barrier((far, tie))
        low_side = jnp.where(my_side == 0, own, far)
        high_side = jnp.where(my_side == 0, far, own)
        both = jnp.stack([low_side, high_side])
        other = swap(both, 1, 0)
        first, second = jnp.where(my_core == 0, both, other), jnp.where(my_core == 0, other, both)
        return jnp.concatenate([first[0], second[0], first[1], second[1]], axis=-1)

    def core_sum(term, section):
        shaped = term.reshape(2, 2, *term.shape[1:])
        keep = lax.dynamic_index_in_dim(shaped, my_core, 1, keepdims=False)
        other = swap(lax.dynamic_index_in_dim(shaped, 1 - my_core, 1, keepdims=False), 1, section)
        pair = keep.astype(jnp.float32) + other.astype(jnp.float32)
        far = lax.dynamic_index_in_dim(pair, 1 - my_side, 0, keepdims=False).astype(jnp.bfloat16)
        return lax.dynamic_index_in_dim(pair, my_side, 0, keepdims=False), far

    def side_sum(own, far, section, tie):
        arrived = swap(far, 2, section)
        if tie is not None:
            arrived, _ = lax.optimization_barrier((arrived, tie))
        return own + arrived.astype(jnp.float32)

    def my_share(array_in):
        return lax.dynamic_slice_in_dim(array_in, my_head * share, share, array_in.ndim - 1)

    def along(array_in, pairs):
        return lax.ppermute(array_in, "frame", pairs)

    at_end = jnp.logical_or(my_frame == 0, my_frame == 3)
    outer, inner = [(0, 1), (1, 0), (2, 3), (3, 2)], [(1, 2), (2, 1)]

    def fetch(shards):
        near = [along(x, outer) for x in shards]
        middle = [along(x, inner) for x in shards]
        across = [along(x, inner) for x in near]
        second = [jnp.where(at_end, along(x, outer), x) for x in middle]
        return near, second, across

    def last_hop(across):
        return jnp.where(at_end, along(across, outer), across)

    if frame_count == 4:
        upper = my_frame // 2
        sources = jnp.stack([my_frame, my_frame + 1 - 2 * (my_frame % 2), 2 - upper, 3 - 3 * upper])
    else:
        sources = jnp.zeros((1,), jnp.int32)
    sources = sources.astype(jnp.int32)

    shards = []
    for chunk in range(chunks):
        cols = slice(chunk * width, (chunk + 1) * width)
        columns = [w_query[0][:, cols], w_key[0][:, cols], w_value[0][:, cols]]
        shards.append(jnp.concatenate(columns, axis=1))
    shards.append(w_out[0])

    saved_space = inputs[0].reshape(batches, rows, feat)
    share_saved = my_share(saved_space)
    if frame_count == 4:
        near, second, across = fetch(shards)
    saved_time = gather_share(place_rows(send_rows(share_saved, leave_space, 0), enter_time))
    saved = jnp.where(on_last, saved_space, saved_time).reshape(batches * rows, feat)
    wide = saved.astype(jnp.float32)
    inv_rms = lax.rsqrt(jnp.mean(wide * wide, axis=-1, keepdims=True) + EPS)
    low = (wide * inv_rms * gain_row).astype(jnp.bfloat16)

    place = jnp.arange(patches) // FRAMES
    mask = jnp.where(on_last, 1.0, (place[:, None] == place[None, :]).astype(jnp.float32))
    raws, pieces = [], []
    if frame_count == 4:
        for chunk in range(chunks):
            pieces.append([shards[chunk], near[chunk], second[chunk], last_hop(across[chunk])])
            raws.append(run_raw(sources, low, pieces[-1]))
        *_, across[-1] = lax.optimization_barrier((*raws[:-1], across[-1]))
        out_pieces = [shards[-1], near[-1], second[-1], last_hop(across[-1])]
    else:
        for chunk in range(chunks):
            pieces.append([lax.all_gather(shards[chunk], "frame", axis=0, tiled=True)])
            raws.append(run_raw(sources, low, pieces[-1]))
        out_pieces = [lax.all_gather(shards[-1], "frame", axis=1, tiled=True)]
    flags = [(lax.axis_index("section") == s).astype(jnp.int32).reshape(1) for s in range(2)]

    def sublayer(flag, grad, first_grad, first, count):
        return run_back(
            flag, sources, mask, gains, inv_rms, gain_row, grad, first_grad, saved, first, count,
            raws, out_pieces, pieces, head_count, head_dim,
        )

    def term_of(section, grad, first_grad, b, tie):
        flag = flags[section]
        if tie is not None:
            flag, _ = lax.optimization_barrier((flag, tie))
        return sublayer(flag, grad, first_grad, b * rows, rows)

    def add(residual, summed):
        return (residual.astype(jnp.float32) + summed).astype(jnp.bfloat16)

    grad_space = upstream.reshape(batches * rows, feat)
    share_space = my_share(upstream.reshape(batches, rows, feat))
    space_parts, sent = [], []
    for b in range(batches):
        tie = space_parts[-1] if b else None
        own, far = core_sum(term_of(1, grad_space, b * rows, b, tie), 1)
        space_parts.append(add(share_space[b], side_sum(own, far, 1, None)))
        sent.append(send_rows(space_parts[-1], leave_space, 1))
    shares, fulls, terms, halves = [], [], [], []
    for b in range(batches):
        if b == 0:
            shares.append(place_rows(sent[b], enter_time)[0])
            fulls.append(gather_share(shares[-1]))
        terms.append(term_of(0, fulls[b], 0, b, halves[-1][1] if b else None))
        halves.append(core_sum(terms[-1], 0))
        if b + 1 < batches:
            arrived, _ = lax.optimization_barrier((sent[b + 1], fulls[b]))
            shares.append(place_rows(arrived, enter_time)[0])
            fulls.append(gather_share(shares[-1], terms[-1]))
    time_parts, returned = [], []
    for b in range(batches):
        tie = terms[b + 1] if b + 1 < batches else None
        part = add(shares[b], side_sum(*halves[b], 0, tie))
        if b:
            part, _ = lax.optimization_barrier((part, returned[-1][0]))
        time_parts.append(part)
        returned.append(send_rows(time_parts[-1], leave_time, 0))
    time_parts = [place_rows(parts, enter_space)[0] for parts in returned]
    result = jnp.where(on_last, jnp.stack(space_parts), jnp.stack(time_parts))
    return result.reshape(1, batches, frames, patches, share)


def solution(mesh):
    in_specs = (
        P("section", None, "frame", None, None),
        P(None, "frame", None, None),
        P("section", None),
        P("section", None, None),
        P("section", "frame", "head"),
        P("section", "frame", "head"),
        P("section", "frame", "head"),
        P("section", "head", "frame"),
    )
    out_specs = P("section", None, "frame", None, "head")
    return jax.shard_map(
        on_device, mesh=mesh, in_specs=in_specs, out_specs=out_specs, check_vma=False
    )
```

```python
import functools

import jax
import jax.numpy as jnp
from jax import lax
from jax.experimental import pallas as pl
from jax.experimental.pallas import tpu as pltpu
from jax.sharding import PartitionSpec as P

FRAMES = 16
EPS = 1e-06


def dot_nn(left, right):
    return lax.dot_general(left, right, (((1,), (0,)), ((), ())), preferred_element_type=jnp.float32)


def dot_nt(left, right):
    return lax.dot_general(left, right, (((1,), (1,)), ((), ())), preferred_element_type=jnp.float32)


def dot_tn(left, right):
    return lax.dot_general(left, right, (((0,), (0,)), ((), ())), preferred_element_type=jnp.float32)


def head_norm(raw_rows):
    scale_rows = lax.rsqrt(jnp.mean(raw_rows * raw_rows, axis=-1, keepdims=True) + EPS)
    return raw_rows * scale_rows, scale_rows


def norm_back(grad_low, normal_hat, scale_rows, gain_vec):
    grad_hat = grad_low.astype(jnp.float32) * gain_vec
    inner_mean = jnp.mean(grad_hat * normal_hat, axis=-1, keepdims=True)
    return (scale_rows * (grad_hat - normal_hat * inner_mean)).astype(jnp.bfloat16)


def attend_back(units, mask):
    scores = [dot_nt(key, query) for query, key, _, _ in units]
    dprobs = [dot_nt(value, grad) for _, _, value, grad in units]
    expo = [jnp.exp(score) * mask for score in scores]
    probs = [x * (1.0 / jnp.sum(x, axis=0, keepdims=True)) for x in expo]
    inner = [jnp.sum(p * d, axis=0, keepdims=True) for p, d in zip(probs, dprobs)]
    dscores = [(p * (d - i)).astype(jnp.bfloat16) for p, d, i in zip(probs, dprobs, inner)]
    dvalues = [dot_nn(p.astype(jnp.bfloat16), unit[3]) for p, unit in zip(probs, units)]
    dkeys = [dot_nn(d, unit[0]) for d, unit in zip(dscores, units)]
    dqueries = [dot_tn(d, unit[1]) for d, unit in zip(dscores, units)]
    return [
        tuple(x.astype(jnp.bfloat16) for x in triple) for triple in zip(dqueries, dkeys, dvalues)
    ]


def raw_kernel(source_ref, low_ref, *refs):
    *piece_refs, raw_ref = refs
    total = None
    for slot, piece_ref in enumerate(piece_refs):
        depth = piece_ref.shape[0]
        start = pl.multiple_of(source_ref[slot] * depth, depth)
        part = dot_nn(low_ref[:, pl.ds(start, depth)], piece_ref[...])
        total = part if total is None else total + part
    raw_ref[...] = total


def run_raw(sources, low, pieces):
    rows, feat = low.shape
    columns = pieces[0].shape[1]
    tile = rows // 4
    once = pl.Buffered(1)
    return pl.pallas_call(
        raw_kernel,
        grid_spec=pltpu.PrefetchScalarGridSpec(
            num_scalar_prefetch=1,
            grid=(rows // tile,),
            in_specs=[pl.BlockSpec((tile, feat), lambda i, source: (i, 0))]
            + [
                pl.BlockSpec(piece.shape, lambda i, source: (0, 0), pipeline_mode=once)
                for piece in pieces
            ],
            out_specs=pl.BlockSpec((tile, columns), lambda i, source: (i, 0)),
        ),
        out_shape=jax.ShapeDtypeStruct((rows, columns), jnp.float32),
        compiler_params=pltpu.CompilerParams(
            dimension_semantics=("arbitrary",), vmem_limit_bytes=40 << 20
        ),
        cost_estimate=pl.CostEstimate(
            flops=2 * rows * feat * columns,
            bytes_accessed=2 * feat * columns + 2 * rows * feat + 4 * rows * columns,
            transcendentals=0,
        ),
        name="raw_products",
    )(sources, low, *pieces)


def back_kernel(chunks, slots, head_dim, first_grad, first_saved, flag_ref, source_ref, *refs):
    @pl.when(flag_ref[0] == 1)
    def _():
        back_body(chunks, slots, head_dim, first_grad, first_saved, source_ref, *refs)


def back_body(chunks, slots, head_dim, first_grad, first_saved, source_ref, *refs):
    (mask_ref, gains_ref, inv_ref, gain_ref, grad_hbm, saved_hbm), refs = refs[:6], refs[6:]
    raw_hbm, refs = refs[:chunks], refs[chunks:]
    out_weight_hbm, refs = refs[:slots], refs[slots:]
    weight_hbm, refs = refs[: chunks * slots], refs[chunks * slots :]
    term_hbm, grad_ref, saved_ref, raw_ref, out_weight_ref, weight_ref = refs[:6]
    total_ref, packed_ref, term_ref, arrived = refs[6:]
    rows, feat = grad_ref.shape
    block = mask_ref.shape[0]
    depth, columns = weight_hbm[0].shape
    width = columns // 3
    places = [pl.multiple_of(source_ref[slot] * depth, depth) for slot in range(slots)]
    started = [0]

    def start(source, target):
        copy = pltpu.make_async_copy(source, target, arrived.at[started[0]])
        started[0] += 1
        copy.start()
        return copy

    get_first = [start(grad_hbm.at[pl.ds(first_grad, rows)], grad_ref)]
    for slot in range(slots):
        target = out_weight_ref.at[:, pl.ds(places[slot], depth)]
        get_first.append(start(out_weight_hbm[slot], target))
    for copy in get_first:
        copy.wait()
    get_raw = [
        start(raw_hbm[chunk].at[pl.ds(first_saved, rows)], raw_ref.at[chunk])
        for chunk in range(chunks)
    ]
    get_rest = []
    for slot in range(slots):
        for chunk in range(chunks):
            target = weight_ref.at[pl.ds(places[slot], depth), pl.ds(chunk * columns, columns)]
            get_rest.append(start(weight_hbm[chunk * slots + slot], target))
    get_rest.append(start(saved_hbm.at[pl.ds(first_saved, rows)], saved_ref))

    query_gain, key_gain = gains_ref[0:1, :], gains_ref[1:2, :]
    mask = mask_ref[...]
    grad_attn = dot_nt(grad_ref[...], out_weight_ref[...]).astype(jnp.bfloat16)
    for chunk in range(chunks):
        get_raw[chunk].wait()
        for head in range(width // head_dim):
            query_cols = slice(head * head_dim, (head + 1) * head_dim)
            key_cols = slice(width + query_cols.start, width + query_cols.stop)
            value_cols = slice(2 * width + query_cols.start, 2 * width + query_cols.stop)
            grad_cols = slice(chunk * width + query_cols.start, chunk * width + query_cols.stop)

            def out_cols(cols):
                return slice(chunk * columns + cols.start, chunk * columns + cols.stop)

            for begin in range(0, rows, 4 * block):
                owns = [
                    slice(first, first + block)
                    for first in range(begin, min(rows, begin + 4 * block), block)
                ]
                queries = [head_norm(raw_ref[chunk, own, query_cols]) for own in owns]
                keys = [head_norm(raw_ref[chunk, own, key_cols]) for own in owns]
                units = [
                    (
                        (query[0] * query_gain).astype(jnp.bfloat16),
                        (key[0] * key_gain).astype(jnp.bfloat16),
                        raw_ref[chunk, own, value_cols].astype(jnp.bfloat16),
                        grad_attn[own, grad_cols],
                    )
                    for own, query, key in zip(owns, queries, keys)
                ]
                backs = attend_back(units, mask)
                for own, query, key, (dquery, dkey, dvalue) in zip(owns, queries, keys, backs):
                    packed_ref[own, out_cols(query_cols)] = norm_back(dquery, *query, query_gain)
                    packed_ref[own, out_cols(key_cols)] = norm_back(dkey, *key, key_gain)
                    packed_ref[own, out_cols(value_cols)] = dvalue
    for copy in get_rest:
        copy.wait()
    shares, _, share_width = term_ref.shape
    packed = packed_ref[...]
    for share in range(shares):
        part = slice(share * share_width, (share + 1) * share_width)
        total_ref[:, part] = dot_nt(packed, weight_ref[part, :])
    sends = []
    for first in range(0, rows, block):
        own = slice(first, first + block)
        inv_rms = inv_ref[first_saved + first : first_saved + first + block, :]
        normed = saved_ref[own, :].astype(jnp.float32) * inv_rms
        grad_hat = total_ref[own, :] * gain_ref[...]
        inner_mean = jnp.mean(grad_hat * normed, axis=-1, keepdims=True)
        term = (inv_rms * (grad_hat - normed * inner_mean)).astype(jnp.bfloat16)
        for share in range(shares):
            term_ref[share, own, :] = term[:, share * share_width : (share + 1) * share_width]
        window = pl.ds(first, block)
        sends.append(start(term_ref.at[:, window], term_hbm.at[:, window]))
    for send in sends:
        send.wait()


def run_back(flag, sources, mask, gains, inv_rms, gain_row, grad, first_grad, saved, first_saved, rows, raws, out_pieces, pieces, shares, head_dim):
    feat = grad.shape[1]
    chunks, slots = len(raws), len(out_pieces)
    columns = pieces[0][0].shape[1]
    heads_width = out_pieces[0].shape[0]
    share_width = feat // shares
    block = mask.shape[0]
    vmem = pl.BlockSpec(memory_space=pltpu.VMEM)
    smem = pl.BlockSpec(memory_space=pltpu.SMEM)
    anywhere = pl.BlockSpec(memory_space=pl.ANY)
    arrays = [grad, saved, *raws, *out_pieces, *(piece for group in pieces for piece in group)]
    copies = len(arrays) + rows // block
    return pl.pallas_call(
        functools.partial(back_kernel, chunks, slots, head_dim, first_grad, first_saved),
        in_specs=[smem] * 2 + [vmem] * 4 + [anywhere] * len(arrays),
        out_specs=anywhere,
        out_shape=jax.ShapeDtypeStruct((shares, rows, share_width), jnp.bfloat16),
        scratch_shapes=[
            pltpu.VMEM((rows, feat), jnp.bfloat16),
            pltpu.VMEM((rows, feat), jnp.bfloat16),
            pltpu.VMEM((chunks, rows, columns), jnp.float32),
            pltpu.VMEM((heads_width, feat), jnp.bfloat16),
            pltpu.VMEM((feat, chunks * columns), jnp.bfloat16),
            pltpu.VMEM((rows, feat), jnp.float32),
            pltpu.VMEM((rows, chunks * columns), jnp.bfloat16),
            pltpu.VMEM((shares, rows, share_width), jnp.bfloat16),
            pltpu.SemaphoreType.DMA((copies,)),
        ],
        compiler_params=pltpu.CompilerParams(vmem_limit_bytes=56 << 20),
        cost_estimate=pl.CostEstimate(
            flops=16 * rows * feat * heads_width,
            bytes_accessed=8 * feat * heads_width + 6 * rows * feat,
            transcendentals=rows * heads_width,
        ),
        name="sublayer_back",
    )(flag, sources, mask, gains, inv_rms, gain_row, *arrays)


def on_device(inputs, upstream, norm_gain, head_gain, w_query, w_key, w_value, w_out):
    on_last = lax.axis_index("section") == 1
    frame_count, head_count = lax.axis_size("frame"), lax.axis_size("head")
    my_frame, my_head = lax.axis_index("frame"), lax.axis_index("head")
    batches, frames, patches, feat = inputs.shape[1:]
    rows = frames * patches
    total_frames = frames * frame_count
    few = patches // frame_count
    piece = frames * few
    head_dim = head_gain.shape[-1]
    share = feat // head_count
    local_width = w_query.shape[2]
    width = 2 * head_dim if local_width % (2 * head_dim) == 0 else head_dim
    chunks = local_width // width
    gain_row = norm_gain
    gains = jnp.stack([head_gain[0, 0] * head_dim ** (-0.5), head_gain[0, 1]])

    def reorder(array_in, source):
        pick = (source[:, None] == jnp.arange(rows)[None, :]).astype(jnp.bfloat16)
        flat = array_in.reshape(-1, rows, array_in.shape[-1])
        moved = jnp.einsum("rs,bsc->brc", pick, flat, preferred_element_type=jnp.float32)
        return moved.astype(jnp.bfloat16)

    index = jnp.arange(rows)
    shift, in_frame, in_few = index // piece, (index % piece) // few, index % few
    target = (my_frame + shift) % frame_count
    leave_space = in_frame * patches + target * few + in_few
    leave_time = in_few * total_frames + target * frames + in_frame
    time_patch, time_frame = index // total_frames, index % total_frames
    enter_time = (
        ((my_frame - time_frame // frames) % frame_count) * piece
        + (time_frame % frames) * few
        + time_patch
    )
    space_frame, space_patch = index // patches, index % patches
    enter_space = (
        ((my_frame - space_patch // few) % frame_count) * piece
        + space_frame * few
        + space_patch % few
    )

    def send_rows(array_in, leave, from_section):
        sorted_rows = reorder(array_in, leave)
        parts = []
        for step in range(frame_count):
            part = sorted_rows[:, step * piece : (step + 1) * piece]
            if step or from_section:
                part = lax.ppermute(
                    part,
                    ("section", "frame"),
                    [
                        (from_section * frame_count + source, (source + step) % frame_count)
                        for source in range(frame_count)
                    ],
                )
            parts.append(part)
        return parts

    def place_rows(parts, enter):
        return reorder(jnp.concatenate(parts, axis=1), enter)

    def swap(array_in, bit, section):
        first = section * head_count
        pairs = [(first + i, first + (i ^ bit)) for i in range(head_count)]
        return lax.ppermute(array_in, ("section", "head"), pairs)

    my_core, my_side = my_head % 2, my_head // 2

    def gather_share(own, tie=None):
        far = swap(own, 2, 0)
        if tie is not None:
            far, _ = lax.optimization_barrier((far, tie))
        low_side = jnp.where(my_side == 0, own, far)
        high_side = jnp.where(my_side == 0, far, own)
        both = jnp.stack([low_side, high_side])
        other = swap(both, 1, 0)
        first, second = jnp.where(my_core == 0, both, other), jnp.where(my_core == 0, other, both)
        return jnp.concatenate([first[0], second[0], first[1], second[1]], axis=-1)

    def core_sum(term, section):
        shaped = term.reshape(2, 2, *term.shape[1:])
        keep = lax.dynamic_index_in_dim(shaped, my_core, 1, keepdims=False)
        other = swap(lax.dynamic_index_in_dim(shaped, 1 - my_core, 1, keepdims=False), 1, section)
        pair = keep.astype(jnp.float32) + other.astype(jnp.float32)
        far = lax.dynamic_index_in_dim(pair, 1 - my_side, 0, keepdims=False).astype(jnp.bfloat16)
        return lax.dynamic_index_in_dim(pair, my_side, 0, keepdims=False), far

    def side_sum(own, far, section, tie):
        arrived = swap(far, 2, section)
        if tie is not None:
            arrived, _ = lax.optimization_barrier((arrived, tie))
        return own + arrived.astype(jnp.float32)

    def my_share(array_in):
        return lax.dynamic_slice_in_dim(array_in, my_head * share, share, array_in.ndim - 1)

    def along(array_in, pairs):
        return lax.ppermute(array_in, "frame", pairs)

    at_end = jnp.logical_or(my_frame == 0, my_frame == 3)
    outer, inner = [(0, 1), (1, 0), (2, 3), (3, 2)], [(1, 2), (2, 1)]

    def fetch(shards):
        near = [along(x, outer) for x in shards]
        middle = [along(x, inner) for x in shards]
        across = [along(x, inner) for x in near]
        second = [jnp.where(at_end, along(x, outer), x) for x in middle]
        return near, second, across

    def last_hop(across):
        return jnp.where(at_end, along(across, outer), across)

    if frame_count == 4:
        upper = my_frame // 2
        sources = jnp.stack([my_frame, my_frame + 1 - 2 * (my_frame % 2), 2 - upper, 3 - 3 * upper])
    else:
        sources = jnp.zeros((1,), jnp.int32)
    sources = sources.astype(jnp.int32)

    shards = []
    for chunk in range(chunks):
        cols = slice(chunk * width, (chunk + 1) * width)
        columns = [w_query[0][:, cols], w_key[0][:, cols], w_value[0][:, cols]]
        shards.append(jnp.concatenate(columns, axis=1))
    shards.append(w_out[0])

    saved_space = inputs[0].reshape(batches, rows, feat)
    share_saved = my_share(saved_space)
    if frame_count == 4:
        near, second, across = fetch(shards)
    saved_time = gather_share(place_rows(send_rows(share_saved, leave_space, 0), enter_time))
    saved = jnp.where(on_last, saved_space, saved_time).reshape(batches * rows, feat)
    wide = saved.astype(jnp.float32)
    inv_rms = lax.rsqrt(jnp.mean(wide * wide, axis=-1, keepdims=True) + EPS)
    low = (wide * inv_rms * gain_row).astype(jnp.bfloat16)

    place = jnp.arange(patches) // FRAMES
    mask = jnp.where(on_last, 1.0, (place[:, None] == place[None, :]).astype(jnp.float32))
    raws, pieces = [], []
    if frame_count == 4:
        for chunk in range(chunks):
            pieces.append([shards[chunk], near[chunk], second[chunk], last_hop(across[chunk])])
            raws.append(run_raw(sources, low, pieces[-1]))
        *_, across[-1] = lax.optimization_barrier((*raws[:-1], across[-1]))
        out_pieces = [shards[-1], near[-1], second[-1], last_hop(across[-1])]
    else:
        for chunk in range(chunks):
            pieces.append([lax.all_gather(shards[chunk], "frame", axis=0, tiled=True)])
            raws.append(run_raw(sources, low, pieces[-1]))
        out_pieces = [lax.all_gather(shards[-1], "frame", axis=1, tiled=True)]
    flags = [(lax.axis_index("section") == s).astype(jnp.int32).reshape(1) for s in range(2)]

    def sublayer(flag, grad, first_grad, first, count):
        return run_back(
            flag, sources, mask, gains, inv_rms, gain_row, grad, first_grad, saved, first, count,
            raws, out_pieces, pieces, head_count, head_dim,
        )

    def term_of(section, grad, first_grad, b, tie):
        flag = flags[section]
        if tie is not None:
            flag, _ = lax.optimization_barrier((flag, tie))
        return sublayer(flag, grad, first_grad, b * rows, rows)

    def add(residual, summed):
        return (residual.astype(jnp.float32) + summed).astype(jnp.bfloat16)

    grad_space = upstream.reshape(batches * rows, feat)
    share_space = my_share(upstream.reshape(batches, rows, feat))
    space_parts, sent = [], []
    for b in range(batches):
        tie = space_parts[-1] if b else None
        own, far = core_sum(term_of(1, grad_space, b * rows, b, tie), 1)
        space_parts.append(add(share_space[b], side_sum(own, far, 1, None)))
        sent.append(send_rows(space_parts[-1], leave_space, 1))
    shares, fulls, time_parts, returned = [], [], [], []
    term = far = None
    for b in range(batches):
        arrived = sent[b]
        if b:
            arrived, _ = lax.optimization_barrier((arrived, term))
        shares.append(place_rows(arrived, enter_time)[0])
        fulls.append(gather_share(shares[-1]))
        term = term_of(0, fulls[b], 0, b, None)
        own, far = core_sum(term, 0)
        time_parts.append(add(shares[b], side_sum(own, far, 0, None)))
        returned.append(send_rows(time_parts[-1], leave_time, 0))
    time_parts = [place_rows(parts, enter_space)[0] for parts in returned]
    result = jnp.where(on_last, jnp.stack(space_parts), jnp.stack(time_parts))
    return result.reshape(1, batches, frames, patches, share)


def solution(mesh):
    in_specs = (
        P("section", None, "frame", None, None),
        P(None, "frame", None, None),
        P("section", None),
        P("section", None, None),
        P("section", "frame", "head"),
        P("section", "frame", "head"),
        P("section", "frame", "head"),
        P("section", "head", "frame"),
    )
    out_specs = P("section", None, "frame", None, "head")
    return jax.shard_map(
        on_device, mesh=mesh, in_specs=in_specs, out_specs=out_specs, check_vma=False
    )
```
